32 devices in a mesh: batch: 8 (over z, x), ctx: 4 (over y, core).
Axes of the slice: x: 2, y: 2, z: 4, core: 2. Of those that a mesh axis runs over, the one named last changes fastest.
Arguments:
- tokens: bfloat16 [8, 512, 2048], P('batch', 'ctx'), may hold values from -6 to 6
- segment_ids: int32 [8, 512], P('batch', 'ctx'), may hold values from 0 to 3, as said below
- positions: int32 [8, 512], P('batch', 'ctx'), may hold values from 0 to 511, as said below
- norm_gain: bfloat16 [1, 2048], P(None, ('batch', 'ctx')), may hold values from 0.5 to 1.5
- norm_bias: bfloat16 [1, 2048], P(None, ('batch', 'ctx')), may hold values from -1 to 1
- qkv_weight: bfloat16 [1, 2048, 6144], P(None, ('batch', 'ctx'))
- qkv_bias: bfloat16 [1, 6144], P(None, ('batch', 'ctx')), may hold values from -1 to 1
- proj_weight: bfloat16 [1, 2048, 2048], P(None, 'ctx', 'batch'), may hold values from -1 to 1
- proj_bias: bfloat16 [1, 2048], P(None, ('batch', 'ctx')), may hold values from -1 to 1
- up_weight: bfloat16 [1, 2048, 8192], P(None, ('batch', 'ctx')), may hold values from -0.125 to 0.125
- up_bias: bfloat16 [1, 8192], P(None, ('batch', 'ctx')), may hold values from -2.5 to 2.5
- down_weight: bfloat16 [1, 8192, 2048], P(None, 'ctx', 'batch'), may hold values from -0.0625 to 0.0625
- down_bias: bfloat16 [1, 2048], P(None, ('batch', 'ctx')), may hold values from -1 to 1
- cotangent: bfloat16 [8, 512, 2048], P('batch', 'ctx'), may hold values from -6 to 6
Outputs:
- block_out: bfloat16 [8, 512, 2048], P('batch', 'ctx')
- grad_tokens: float32 [8, 512, 2048], P('batch', 'ctx')
- grad_norm_gain: float32 [1, 2048], P(None, ('batch', 'ctx'))
- grad_norm_bias: float32 [1, 2048], P(None, ('batch', 'ctx'))
- grad_qkv_weight: float32 [1, 2048, 6144], P(None, ('batch', 'ctx'))
- grad_qkv_bias: float32 [1, 6144], P(None, ('batch', 'ctx'))
- grad_proj_weight: float32 [1, 2048, 2048], P(None, 'ctx', 'batch')
- grad_proj_bias: float32 [1, 2048], P(None, ('batch', 'ctx'))
- grad_up_weight: float32 [1, 2048, 8192], P(None, ('batch', 'ctx'))
- grad_up_bias: float32 [1, 8192], P(None, ('batch', 'ctx'))
- grad_down_weight: float32 [1, 8192, 2048], P(None, 'ctx', 'batch')
- grad_down_bias: float32 [1, 2048], P(None, ('batch', 'ctx'))
The draws below stay inside these ranges and needn't reach their ends.
Inputs may be any that keep to these rules, and one draw needn't show every extreme that they name: `segment_ids`: segment ids never fall along a sequence; at most 4 documents a sequence; some sequence is one whole document. `positions`: A token's position is the number of tokens before it in its document.
All inputs are finite; a program needn't handle non-finite values.
Results may differ from the reference program's by a relative error of at most 0.014.
Values may be sent and summed in bfloat16 or wider, within the bound.
No kernel may reach another device: no remote copies, remote signals or barrier semaphores. Data moves between devices by JAX's collectives and lax.ppermute only.
A program may use at most 192 MiB of HBM per device.

```python
import math
import jax
import jax.numpy as jnp
from jax import lax

D = 2048
HEADS = 32
HEAD_DIM = 64
ROT = 32
FF = 8192
LAYERS = 1
SEQ_LEN = 512
DOCS = 4
SEQS = 8


def cut_table(key):
    folded = jax.random.fold_in(key, 7)
    cut_points = jax.random.randint(folded, (SEQS, DOCS - 1), 1, SEQ_LEN, dtype=jnp.int32)
    is_first = jnp.arange(SEQS, dtype=jnp.int32)[:, None] == 0
    return jnp.where(is_first, SEQ_LEN, cut_points)


def draw_segment_ids(key, part):
    cut_points = cut_table(key)
    token_place = jnp.arange(SEQ_LEN, dtype=jnp.int32)
    passed = token_place[None, :, None] >= cut_points[:, None, :]
    return jnp.sum(passed.astype(jnp.int32), axis=-1).astype(jnp.int32)


def draw_positions(key, part):
    cut_points = cut_table(key)
    token_place = jnp.arange(SEQ_LEN, dtype=jnp.int32)
    passed = token_place[None, :, None] >= cut_points[:, None, :]
    doc_start = jnp.max(jnp.where(passed, cut_points[:, None, :], 0), axis=-1)
    return (token_place[None, :] - doc_start).astype(jnp.int32)


def draw_qkv_weight(key, part):
    full_shape = (LAYERS, D, 3 * D)
    values = jnp.clip(jax.random.normal(key, full_shape, jnp.float32), -6.0, 6.0) * (1.0 / math.sqrt(D))
    return values.astype(jnp.bfloat16)


def block_scale(key, shape, pieces, low, largest):
    def one(dim, blocks):
        heights = jax.random.uniform(jax.random.fold_in(jax.random.fold_in(key, 6), dim), (blocks,), jnp.float32, low / len(pieces), largest / len(pieces))
        return jnp.repeat(jnp.exp(heights), shape[dim] // blocks).reshape((-1,) + (1,) * (len(shape) - dim - 1))

    gain = one(*pieces[0])
    for cut in pieces[1:]:
        gain = gain * one(*cut)
    return gain


def centred(key, extent, deviation, limit, pieces=(), kind=jnp.bfloat16):
    values = jax.random.normal(key, extent, jnp.float32) * deviation
    if len(pieces) > 0:
        values = block_scale(key, extent, pieces, -0.22, 0.18) * values
    return jnp.clip(values, min=-limit, max=limit).astype(kind)


def setup_inputs(seed: int = 0) -> dict:
    arg_keys = jax.random.split(jax.random.key(seed), 15)
    return {
        "tokens": centred(arg_keys[0], (SEQS, SEQ_LEN, D), 1.0, 6.0, ((0, 8), (1, 4))),
        "segment_ids": draw_segment_ids(jax.random.fold_in(arg_keys[14], 71), 0),
        "positions": draw_positions(jax.random.fold_in(arg_keys[14], 71), 0),
        "norm_gain": jnp.clip(1.0 + 0.1 * jax.random.normal(arg_keys[3], (LAYERS, D), jnp.float32), 0.5, 1.5).astype(jnp.bfloat16),
        "norm_bias": centred(arg_keys[4], (LAYERS, D), 0.2, 1.0, ((1, 32),)),
        "qkv_weight": draw_qkv_weight(jax.random.fold_in(arg_keys[14], 71), 0),
        "qkv_bias": centred(arg_keys[6], (LAYERS, 3 * D), 0.2, 1.0, ((1, 32),)),
        "proj_weight": centred(arg_keys[7], (LAYERS, D, D), (D // 64) ** -0.5, 1.0, ((1, 4), (2, 8))),
        "proj_bias": centred(arg_keys[8], (LAYERS, D), 0.2, 1.0, ((1, 32),)),
        "up_weight": centred(arg_keys[9], (LAYERS, D, FF), D ** -0.5, 0.125, ((1, 32),)),
        "up_bias": centred(arg_keys[10], (LAYERS, FF), 0.5, 2.5, ((1, 32),)),
        "down_weight": centred(arg_keys[11], (LAYERS, FF, D), FF ** -0.5, 0.0625, ((1, 4), (2, 8))),
        "down_bias": centred(arg_keys[12], (LAYERS, D), 0.2, 1.0, ((1, 32),)),
        "cotangent": centred(arg_keys[13], (SEQS, SEQ_LEN, D), 1.0, 6.0, ((0, 8), (1, 4))),
    }


EPSILON = 1e-05
MASKED = -1e+30

def norm_rows(residual, gain_row, shift_row):
    average = lax.optimization_barrier(jnp.mean(residual, axis=-1, keepdims=True))
    centered = residual - average
    variance = lax.optimization_barrier(jnp.mean(centered * centered, axis=-1, keepdims=True))
    inverse = lax.rsqrt(variance + EPSILON)
    standard = centered * inverse
    normed = (standard * gain_row.astype(jnp.float32) + shift_row.astype(jnp.float32)).astype(jnp.bfloat16)
    return (standard, inverse, normed)

def rotary_tables(positions):
    half_rot = ROT // 2
    counter = jnp.arange(half_rot, dtype=jnp.float32)
    frequency = jnp.exp(counter * (-2.0 * math.log(10000.0) / ROT))
    phases = positions.astype(jnp.float32)[..., None] * frequency
    return (jnp.cos(phases), jnp.sin(phases))

def rotate(tensor, cos_table, sin_table, direction):
    half_rot = ROT // 2
    cos_part = cos_table[..., None, :]
    sin_part = sin_table[..., None, :] * direction
    leading = tensor[..., :half_rot]
    trailing = tensor[..., half_rot:ROT]
    return jnp.concatenate([leading * cos_part - trailing * sin_part, trailing * cos_part + leading * sin_part, tensor[..., ROT:]], axis=-1)

def split_heads(tensor):
    return tensor.reshape(tensor.shape[:-1] + (HEADS, HEAD_DIM))

def gelu_back(before, upstream):
    return jax.vjp(lambda argument: jax.nn.gelu(argument, approximate=True), before)[1](upstream)[0]

def sequence_mask(segments):
    counter = jnp.arange(segments.shape[0], dtype=jnp.int32)
    return (segments[:, None] == segments[None, :]) & (counter[None, :] <= counter[:, None])

def masked_scores(queries, key_rows, allowed):
    score_scale = 1.0 / math.sqrt(HEAD_DIM)
    scores = jnp.einsum('qhd,khd->hqk', queries.astype(jnp.float32), key_rows.astype(jnp.float32)) * score_scale
    return jnp.where(allowed[None], scores, MASKED)

def attend(queries, key_rows, value_rows, segments):
    scores = masked_scores(queries, key_rows, sequence_mask(segments))
    row_max = lax.optimization_barrier(jnp.max(scores, axis=-1, keepdims=True))
    exponent = jnp.exp(scores - row_max)
    row_total = lax.optimization_barrier(jnp.sum(exponent, axis=-1, keepdims=True))
    weights = (exponent / row_total).astype(jnp.bfloat16)
    log_total = row_max + jnp.log(row_total)
    attended = jnp.einsum('hqk,khd->qhd', weights.astype(jnp.float32), value_rows.astype(jnp.float32)).astype(jnp.bfloat16)
    return (attended, log_total)

def attend_back(queries, key_rows, value_rows, segments, attended, log_total, upstream):
    score_scale = 1.0 / math.sqrt(HEAD_DIM)
    scores = masked_scores(queries, key_rows, sequence_mask(segments))
    probabilities = jnp.exp(scores - log_total)
    rounded = probabilities.astype(jnp.bfloat16)
    grad_value = jnp.einsum('hqk,qhd->khd', rounded.astype(jnp.float32), upstream.astype(jnp.float32))
    grad_probs = jnp.einsum('qhd,khd->hqk', upstream.astype(jnp.float32), value_rows.astype(jnp.float32))
    agreement = lax.optimization_barrier(jnp.sum(upstream.astype(jnp.float32) * attended.astype(jnp.float32), axis=-1))
    grad_scores = (probabilities * (grad_probs - jnp.transpose(agreement)[:, :, None]) * score_scale).astype(jnp.bfloat16)
    grad_query = jnp.einsum('hqk,khd->qhd', grad_scores.astype(jnp.float32), key_rows.astype(jnp.float32))
    grad_key = jnp.einsum('hqk,qhd->khd', grad_scores.astype(jnp.float32), queries.astype(jnp.float32))
    return (grad_query, grad_key, grad_value)

def layer_forward(residual, segments, cos_table, sin_table, params):
    norm_gain, norm_bias, qkv_weight, qkv_bias, proj_weight, proj_bias, up_weight, up_bias, down_weight, down_bias = params
    standard, inverse, normed = norm_rows(residual, norm_gain, norm_bias)
    normed_rows = normed.reshape(-1, D)
    mixed_proj = jnp.dot(normed_rows, qkv_weight, preferred_element_type=jnp.float32) + qkv_bias.astype(jnp.float32)
    mixed_proj = mixed_proj.reshape(residual.shape[:-1] + (3 * D,))
    queries = rotate(split_heads(mixed_proj[..., :D]), cos_table, sin_table, 1.0).astype(jnp.bfloat16)
    key_rows = rotate(split_heads(mixed_proj[..., D:2 * D]), cos_table, sin_table, 1.0).astype(jnp.bfloat16)
    value_rows = split_heads(mixed_proj[..., 2 * D:]).astype(jnp.bfloat16)
    attended, log_total = lax.map(lambda entries: attend(entries[0], entries[1], entries[2], entries[3]), (queries, key_rows, value_rows, segments))
    projected = jnp.dot(attended.reshape(-1, D), proj_weight, preferred_element_type=jnp.float32) + proj_bias.astype(jnp.float32)
    before = jnp.dot(normed_rows, up_weight, preferred_element_type=jnp.float32) + up_bias.astype(jnp.float32)
    activated = jax.nn.gelu(before, approximate=True).astype(jnp.bfloat16)
    lowered = jnp.dot(activated, down_weight, preferred_element_type=jnp.float32) + down_bias.astype(jnp.float32)
    updated = residual + (projected + lowered).reshape(residual.shape)
    stored = (standard, inverse, normed_rows, queries, key_rows, value_rows, attended, log_total, before, activated)
    return (updated, stored)

def layer_backward(gradient, segments, cos_table, sin_table, params, stored):
    norm_gain, norm_bias, qkv_weight, qkv_bias, proj_weight, proj_bias, up_weight, up_bias, down_weight, down_bias = params
    standard, inverse, normed_rows, queries, key_rows, value_rows, attended, log_total, before, activated = stored
    flat_grad = gradient.reshape(-1, D)
    grad_rows = flat_grad.astype(jnp.bfloat16)
    bias_grad = lax.optimization_barrier(jnp.sum(flat_grad, axis=0))
    grad_down = jnp.dot(activated.T, grad_rows, preferred_element_type=jnp.float32)
    grad_act = jnp.dot(grad_rows, down_weight.T, preferred_element_type=jnp.float32)
    grad_before = gelu_back(before, grad_act)
    grad_up_bias = lax.optimization_barrier(jnp.sum(grad_before, axis=0))
    before_rows = grad_before.astype(jnp.bfloat16)
    grad_up = jnp.dot(normed_rows.T, before_rows, preferred_element_type=jnp.float32)
    grad_normed = jnp.dot(before_rows, up_weight.T, preferred_element_type=jnp.float32)
    grad_proj = jnp.dot(attended.reshape(-1, D).T, grad_rows, preferred_element_type=jnp.float32)
    grad_attended = jnp.dot(grad_rows, proj_weight.T, preferred_element_type=jnp.float32).astype(jnp.bfloat16).reshape(attended.shape)
    grad_query, grad_key, grad_value = lax.map(lambda entries: attend_back(entries[0], entries[1], entries[2], entries[3], entries[4], entries[5], entries[6]), (queries, key_rows, value_rows, segments, attended, log_total, grad_attended))
    grad_query = rotate(grad_query, cos_table, sin_table, -1.0).reshape(gradient.shape)
    grad_key = rotate(grad_key, cos_table, sin_table, -1.0).reshape(gradient.shape)
    grad_mixed = jnp.concatenate([grad_query, grad_key, grad_value.reshape(gradient.shape)], axis=-1).reshape(-1, 3 * D)
    grad_qkv_bias = lax.optimization_barrier(jnp.sum(grad_mixed, axis=0))
    mixed_rows = grad_mixed.astype(jnp.bfloat16)
    grad_qkv = jnp.dot(normed_rows.T, mixed_rows, preferred_element_type=jnp.float32)
    grad_normed = (grad_normed + jnp.dot(mixed_rows, qkv_weight.T, preferred_element_type=jnp.float32)).reshape(gradient.shape)
    grad_gain = lax.optimization_barrier(jnp.sum((grad_normed * standard).reshape(-1, D), axis=0))
    grad_shift = lax.optimization_barrier(jnp.sum(grad_normed.reshape(-1, D), axis=0))
    scaled = grad_normed * norm_gain.astype(jnp.float32)
    grad_input = inverse * (scaled - lax.optimization_barrier(jnp.mean(scaled, axis=-1, keepdims=True)) - standard * lax.optimization_barrier(jnp.mean(scaled * standard, axis=-1, keepdims=True)))
    layer_grads = (grad_gain, grad_shift, grad_qkv, grad_qkv_bias, grad_proj, bias_grad, grad_up, grad_up_bias, grad_down, bias_grad)
    return (gradient + grad_input, layer_grads)

def reference(tokens, segment_ids, positions, norm_gain, norm_bias, qkv_weight, qkv_bias, proj_weight, proj_bias, up_weight, up_bias, down_weight, down_bias, cotangent):
    weights_all = (norm_gain, norm_bias, qkv_weight, qkv_bias, proj_weight, proj_bias, up_weight, up_bias, down_weight, down_bias)
    group_size = math.gcd(SEQS, max(1, 4096 // SEQ_LEN))
    blocks = SEQS // group_size

    def one_block(totals, block_entry):
        block_tokens, block_segments, block_positions, block_cotangent = block_entry
        cos_table, sin_table = rotary_tables(block_positions)
        residual = block_tokens.astype(jnp.float32)
        stored_list = []
        for layer_index in range(LAYERS):
            params = tuple((member[layer_index] for member in weights_all))
            residual, stored = layer_forward(residual, block_segments, cos_table, sin_table, params)
            stored_list.append(stored)
        gradient = block_cotangent.astype(jnp.float32)
        per_layer = list(range(LAYERS))
        for layer_index in reversed(range(LAYERS)):
            params = tuple((member[layer_index] for member in weights_all))
            gradient, layer_grads = layer_backward(gradient, block_segments, cos_table, sin_table, params, stored_list[layer_index])
            per_layer[layer_index] = layer_grads
        updated = tuple((running + jnp.stack([per_layer[layer_index][member] for layer_index in range(LAYERS)]) for member, running in enumerate(totals)))
        return (updated, (residual.astype(jnp.bfloat16), gradient))
    initial = tuple((jnp.zeros(member.shape, jnp.float32) for member in weights_all))
    inputs = (tokens.reshape(blocks, group_size, SEQ_LEN, D), segment_ids.reshape(blocks, group_size, SEQ_LEN), positions.reshape(blocks, group_size, SEQ_LEN), cotangent.reshape(blocks, group_size, SEQ_LEN, D))
    totals, (outputs, gradients) = lax.scan(one_block, initial, inputs)
    return (outputs.reshape(SEQS, SEQ_LEN, D), gradients.reshape(SEQS, SEQ_LEN, D), totals[0], totals[1], totals[2], totals[3], totals[4], totals[5], totals[6], totals[7], totals[8], totals[9])
```

```python
import math

import jax
import jax.numpy as jnp
from jax import lax
from jax.sharding import Mesh
from jax.sharding import PartitionSpec as P

D = 2048
HEAD_DIM = 64
ROT = 32
FF = 8192
LANES = 128

EPSILON = 1e-05
MASKED = -1e30


F32 = jnp.float32
BF16 = jnp.bfloat16


def bits_of(axis):
    size = lax.axis_size(axis)
    return [1 << place for place in range(size.bit_length() - 1)]


def swap(value, axis, mask):
    size = lax.axis_size(axis)
    return lax.ppermute(value, axis, [(place, place ^ mask) for place in range(size)])


def ordered(parts, axis):
    me = lax.axis_index(axis)
    parts = list(parts)
    for bit in bits_of(axis):
        odd = (me & bit) != 0
        parts = [jnp.where(odd, parts[k ^ bit], parts[k]) for k in range(len(parts))]
    return parts


def relative(stack, axis, dim):
    size = lax.axis_size(axis)
    return jnp.stack(ordered([lax.index_in_dim(stack, k, dim, keepdims=False) for k in range(size)], axis), dim)


def pick(stack, axis, mask, dim):
    me = lax.axis_index(axis)
    return lax.dynamic_index_in_dim(stack, me ^ mask, dim, keepdims=False)


def gather_small(value, axes):
    value = value[None]
    for axis in reversed(axes):
        for bit in bits_of(axis):
            other = swap(value, axis, bit)
            odd = (lax.axis_index(axis) & bit) != 0
            value = jnp.concatenate(
                [jnp.where(odd, other, value), jnp.where(odd, value, other)], axis=0
            )
    return value


def add_small(value, axes):
    for axis in axes:
        for bit in bits_of(axis):
            value = value + swap(value, axis, bit)
    return value


def gather_rows(value):
    pieces = {0: value}
    for bit in reversed(bits_of("bo")):
        for place in list(pieces):
            pieces[place | bit] = swap(pieces[place], "bo", bit)
    chunks = []
    for place in range(lax.axis_size("bo")):
        rows = [pieces[place]]
        for axis in ("cy", "cc"):
            for bit in bits_of(axis):
                rows = rows + [swap(row, axis, bit) for row in rows]
        chunks.append(rows)
    return chunks


def scatter_rows(chunk_rows):
    summed = []
    for rows in chunk_rows:
        for axis in ("cc", "cy"):
            for bit in reversed(bits_of(axis)):
                half = rows.shape[0] // 2
                rows = (
                    rows[:half].astype(F32) + swap(rows[half:], axis, bit).astype(F32)
                ).astype(BF16)
        summed.append(rows[0])
    for bit in bits_of("bo"):
        kept = {}
        step = bit * 2
        for place in range(0, len(summed), step):
            arrived = swap(summed[place + bit], "bo", bit)
            kept[place] = summed[place].astype(F32) + arrived.astype(F32)
            if step < len(summed):
                kept[place] = kept[place].astype(BF16)
        summed = [kept.get(place) for place in range(len(summed))]
    return summed[0]


def spread_columns(stack):
    parts = [pick(stack, "bo", 0, 1)]
    for mask in range(1, lax.axis_size("bo")):
        parts.append(swap(pick(stack, "bo", mask, 1), "bo", mask))
    stack = jnp.stack(ordered(parts, "bo"))
    for dim, axis in ((2, "cy"), (3, "cc")):
        size = lax.axis_size(axis)
        parts = [pick(stack, axis, 0, dim)]
        for mask in range(1, size):
            parts.append(swap(pick(stack, axis, mask, dim), axis, mask))
        stack = jnp.stack(ordered(parts, axis))
        if axis == "cy":
            stack = stack.transpose(1, 2, 0, 3, 4)[:, :, :, :, :]
            stack = stack.transpose(0, 1, 2, 3, 4)
    stack = stack.transpose(1, 3, 0, 2, 4)
    parts = [stack]
    for mask in range(1, lax.axis_size("bi")):
        parts.append(swap(stack, "bi", mask))
    return jnp.stack(ordered(parts, "bi"), 1)


def return_columns(grad):
    total = pick(grad, "bi", 0, 1)
    for mask in range(1, lax.axis_size("bi")):
        total = total + swap(pick(grad, "bi", mask, 1).astype(BF16), "bi", mask).astype(F32)
    stack = total.astype(BF16)
    for dim, axis in ((2, "cc"), (2, "cy"), (2, "bo")):
        parts = [pick(stack, axis, 0, dim)]
        for mask in range(1, lax.axis_size(axis)):
            parts.append(swap(pick(stack, axis, mask, dim), axis, mask))
        stack = jnp.stack(ordered(parts, axis))
    return stack


def norm_rows(residual, gain_row, shift_row):
    average = jnp.mean(residual, axis=-1, keepdims=True)
    centered = residual - average
    variance = jnp.mean(centered * centered, axis=-1, keepdims=True)
    inverse = lax.rsqrt(variance + EPSILON)
    standard = centered * inverse
    normed = (standard * gain_row + shift_row).astype(BF16)
    return (standard, inverse, normed)


def norm_back(grad_normed, standard, inverse, gain_row):
    grad_gain = jnp.sum(grad_normed * standard, axis=0)
    grad_shift = jnp.sum(grad_normed, axis=0)
    scaled = grad_normed * gain_row
    grad_input = inverse * (
        scaled
        - jnp.mean(scaled, axis=-1, keepdims=True)
        - standard * jnp.mean(scaled * standard, axis=-1, keepdims=True)
    )
    return (grad_gain, grad_shift, grad_input)


def rotary_tables(positions):
    half_rot = ROT // 2
    counter = jnp.arange(half_rot, dtype=F32)
    frequency = jnp.exp(counter * (-2.0 * math.log(10000.0) / ROT))
    phases = positions[..., None] * frequency
    return (jnp.cos(phases), jnp.sin(phases))


def rotate(tensor, cos_table, sin_table, direction):
    half_rot = ROT // 2
    cos_part = cos_table[..., None, :]
    sin_part = sin_table[..., None, :] * direction
    leading = tensor[..., :half_rot]
    trailing = tensor[..., half_rot:ROT]
    return jnp.concatenate(
        [
            leading * cos_part - trailing * sin_part,
            trailing * cos_part + leading * sin_part,
            tensor[..., ROT:],
        ],
        axis=-1,
    )


def gelu_back(before, upstream):
    return jax.vjp(lambda argument: jax.nn.gelu(argument, approximate=True), before)[1](upstream)[0]


def masked_scores(queries, key_all, allowed):
    score_scale = 1.0 / math.sqrt(HEAD_DIM)
    scores = (
        jnp.einsum("sqhd,skhd->shqk", queries, key_all, preferred_element_type=F32) * score_scale
    )
    return jnp.where(allowed, scores, MASKED)


def attention_forward(queries, key_all, value_all, allowed):
    scores = masked_scores(queries, key_all, allowed)
    row_max = jnp.max(scores, axis=-1, keepdims=True)
    exponent = jnp.exp(scores - row_max)
    row_total = jnp.sum(exponent, axis=-1, keepdims=True)
    weights = (exponent / row_total).astype(BF16)
    log_total = row_max + jnp.log(row_total)
    attended = jnp.einsum(
        "shqk,skhd->sqhd", weights, value_all, preferred_element_type=F32
    ).astype(BF16)
    return (attended, log_total)


def attention_backward(queries, key_all, value_all, allowed, attended, log_total, grad_attended):
    score_scale = 1.0 / math.sqrt(HEAD_DIM)
    scores = masked_scores(queries, key_all, allowed)
    probabilities = jnp.exp(scores - log_total)
    rounded = probabilities.astype(BF16)
    grad_value = jnp.einsum("shqk,sqhd->skhd", rounded, grad_attended, preferred_element_type=F32)
    grad_probs = jnp.einsum("sqhd,skhd->shqk", grad_attended, value_all, preferred_element_type=F32)
    agreement = jnp.sum(grad_attended.astype(F32) * attended.astype(F32), axis=-1)
    grad_scores = (
        probabilities * (grad_probs - jnp.transpose(agreement, (0, 2, 1))[..., None]) * score_scale
    ).astype(BF16)
    grad_query = jnp.einsum("shqk,skhd->sqhd", grad_scores, key_all, preferred_element_type=F32)
    grad_key = jnp.einsum("shqk,sqhd->skhd", grad_scores, queries, preferred_element_type=F32)
    return (grad_query, grad_key, grad_value)


def dot(left, right):
    return jnp.dot(left, right, preferred_element_type=F32)


def body(
    tokens,
    segment_ids,
    positions,
    norm_gain,
    norm_bias,
    qkv_weight,
    qkv_bias,
    proj_weight,
    proj_bias,
    up_weight,
    up_bias,
    down_weight,
    down_bias,
    cotangent,
):
    n_bo, n_bi = lax.axis_size("bo"), lax.axis_size("bi")
    n_cy, n_cc = lax.axis_size("cy"), lax.axis_size("cc")
    n_ctx = n_cy * n_cc
    bo, bi, cy, cc = (lax.axis_index(axis) for axis in ("bo", "bi", "cy", "cc"))
    every = ("bo", "bi", "cy", "cc")
    sequences, rows, _ = tokens.shape
    weight_rows = qkv_weight.shape[1]
    width = D // (n_bo * n_ctx)
    share = FF // (n_bo * n_ctx)
    heads = width // HEAD_DIM
    full_len = rows * n_ctx
    plane = n_bo * sequences

    vectors = (norm_gain, norm_bias, qkv_bias, proj_bias, up_bias, down_bias)
    small = [vector.reshape(-1).astype(F32) for vector in vectors]
    small += [segment_ids.reshape(-1).astype(F32), positions.reshape(-1).astype(F32)]
    sizes = [part.shape[0] for part in small]
    table = gather_small(jnp.concatenate(small), every)
    columns = []
    start = 0
    for size in sizes:
        columns.append(lax.slice_in_dim(table, start, start + size, axis=1))
        start += size
    gain_row, shift_row, qkv_bias_all, proj_bias_all, up_bias_all, down_bias_all = (
        column.reshape(-1) for column in columns[:6]
    )
    qkv_bias_mine = lax.dynamic_slice(
        qkv_bias_all.reshape(3, n_ctx, n_bo, width),
        (0, cy * n_cc + cc, bo, 0),
        (3, 1, 1, width),
    ).reshape(3 * width)
    up_bias_mine = lax.dynamic_slice_in_dim(
        up_bias_all, ((cy * n_cc + cc) * n_bo + bo) * share, share
    )

    def labels(column):
        value = column.reshape(n_bo, n_bi, n_cy, n_cc, sequences, rows)
        value = pick(value, "bi", 0, 1)
        value = relative(relative(relative(value, "bo", 0), "cy", 1), "cc", 2)
        return value.transpose(0, 3, 2, 1, 4).reshape(plane, full_len)

    segments, places_in_doc = labels(columns[6]), labels(columns[7])
    quarter = (cy ^ jnp.arange(n_cy))[None, :] * n_cc + (cc ^ jnp.arange(n_cc))[:, None]
    place = (quarter.reshape(-1)[:, None] * rows + jnp.arange(rows)[None, :]).reshape(full_len)
    allowed = (segments[:, :, None] == segments[:, None, :]) & (
        place[None, None, :] <= place[None, :, None]
    )
    allowed = allowed[:, None]
    cos_table, sin_table = rotary_tables(places_in_doc)

    qkv_local = qkv_weight.reshape(weight_rows, 3, n_cy, n_cc, n_bo, width)
    qkv_local = qkv_local.transpose(0, 4, 2, 3, 1, 5).reshape(weight_rows, n_bo, n_cy, n_cc, 3 * width)
    qkv_mine = spread_columns(qkv_local).reshape(D, 3 * width)
    up_local = up_weight.reshape(weight_rows, n_cy, n_cc, n_bo, share).transpose(0, 3, 1, 2, 4)
    up_mine = spread_columns(up_local).reshape(D, share)
    out_columns = proj_weight.shape[2]
    out_local = jnp.concatenate(
        [
            proj_weight.reshape(n_bo, width, out_columns),
            down_weight.reshape(n_bo, share, out_columns),
        ],
        axis=1,
    )
    parts = [pick(out_local, "bo", 0, 0)]
    for mask in range(1, n_bo):
        parts.append(swap(pick(out_local, "bo", mask, 0), "bo", mask))
    out_stack = jnp.stack(ordered(parts, "bo"))
    parts = [out_stack]
    for mask in range(1, n_bi):
        parts.append(swap(out_stack, "bi", mask))
    out_mine = jnp.stack(ordered(parts, "bi"), 1)
    out_mine = out_mine.transpose(2, 0, 1, 3).reshape(width + share, D)

    local_rows = sequences * rows
    residual = tokens.astype(F32).reshape(local_rows, D)
    standard, inverse, normed = norm_rows(residual, gain_row, shift_row)

    def all_rows(value):
        chunks = gather_rows(value)
        if sequences == 1:
            return jnp.concatenate([row for chunk in chunks for row in chunk], axis=0)
        stacked = jnp.stack([jnp.stack(chunk) for chunk in chunks])
        stacked = stacked.reshape(n_bo, n_ctx, sequences, rows, D).transpose(0, 2, 1, 3, 4)
        return stacked.reshape(plane * full_len, D)

    def own_rows(value):
        value = value.astype(BF16).reshape(n_bo, sequences, n_ctx, rows, D)
        if sequences > 1:
            value = value.transpose(0, 2, 1, 3, 4)
        value = value.reshape(n_bo, n_ctx, local_rows, D)
        return scatter_rows([value[k] for k in range(n_bo)])

    normed_all = all_rows(normed)
    grad_all = all_rows(cotangent.reshape(local_rows, D))

    mixed = dot(normed_all, qkv_mine) + qkv_bias_mine
    mixed = mixed.reshape(plane, full_len, 3, heads, HEAD_DIM)
    queries = rotate(mixed[:, :, 0], cos_table, sin_table, 1.0).astype(BF16)
    key_all = rotate(mixed[:, :, 1], cos_table, sin_table, 1.0).astype(BF16)
    value_all = mixed[:, :, 2].astype(BF16)
    attended, log_total = attention_forward(queries, key_all, value_all, allowed)
    before = dot(normed_all, up_mine) + up_bias_mine
    activated = jax.nn.gelu(before, approximate=True).astype(BF16)
    inner = jnp.concatenate([attended.reshape(-1, width), activated], axis=1)
    summed = own_rows(dot(inner, out_mine))
    updated = residual + (summed + proj_bias_all + down_bias_all)

    grad_out = dot(inner.T, grad_all)
    grad_inner = dot(grad_all, out_mine.T)
    grad_attended = grad_inner[:, :width].astype(BF16).reshape(attended.shape)
    grad_before = gelu_back(before, grad_inner[:, width:])
    grad_up_bias = jnp.sum(grad_before, axis=0)
    before_rows = grad_before.astype(BF16)
    grad_up = dot(normed_all.T, before_rows)
    grad_query, grad_key, grad_value = attention_backward(
        queries, key_all, value_all, allowed, attended, log_total, grad_attended
    )
    grad_query = rotate(grad_query, cos_table, sin_table, -1.0)
    grad_key = rotate(grad_key, cos_table, sin_table, -1.0)
    grad_mixed = jnp.stack([grad_query, grad_key, grad_value], axis=2).reshape(-1, 3 * width)
    grad_qkv_bias = jnp.sum(grad_mixed, axis=0)
    mixed_rows = grad_mixed.astype(BF16)
    grad_qkv = dot(normed_all.T, mixed_rows)
    grad_normed = own_rows(dot(mixed_rows, qkv_mine.T) + dot(before_rows, up_mine.T))
    grad_gain, grad_shift, grad_input = norm_back(grad_normed, standard, inverse, gain_row)
    grad_tokens = cotangent.astype(F32).reshape(local_rows, D) + grad_input

    spread = (n_bo, n_bi, n_cy, n_cc, weight_rows)
    owner_qkv = return_columns(grad_qkv.reshape(spread + (3 * width,)))
    owner_qkv = owner_qkv.reshape(n_bo, n_ctx, weight_rows, 3, width).transpose(2, 3, 1, 0, 4)
    owner_qkv = owner_qkv.reshape(weight_rows, 3 * D).astype(F32)
    owner_up = return_columns(grad_up.reshape(spread + (share,)))
    owner_up = owner_up.reshape(n_bo, n_ctx, weight_rows, share).transpose(2, 1, 0, 3)
    owner_up = owner_up.reshape(weight_rows, FF).astype(F32)
    grad_out = grad_out.reshape(width + share, n_bo, n_bi, out_columns)
    total = pick(grad_out, "bi", 0, 2)
    for mask in range(1, n_bi):
        total = total + swap(pick(grad_out, "bi", mask, 2).astype(BF16), "bi", mask).astype(F32)
    total = total.astype(BF16)
    parts = [pick(total, "bo", 0, 1)]
    for mask in range(1, n_bo):
        parts.append(swap(pick(total, "bo", mask, 1), "bo", mask))
    owner_out = jnp.stack(ordered(parts, "bo")).astype(F32)
    owner_proj = owner_out[:, :width].reshape(n_bo * width, out_columns)
    owner_down = owner_out[:, width:].reshape(n_bo * share, out_columns)

    linear = ((bo * n_bi + bi) * n_cy + cy) * n_cc + cc
    column_sums = add_small(jnp.concatenate([grad_qkv_bias, grad_up_bias]), ("bi",))
    column_sums = gather_small(column_sums, ("bo", "cy", "cc"))
    qkv_sums = column_sums[:, : 3 * width].reshape(n_bo, n_ctx, 3, width).transpose(2, 1, 0, 3)
    up_sums = column_sums[:, 3 * width :].reshape(n_bo, n_ctx, share).transpose(1, 0, 2)
    owner_qkv_bias = lax.dynamic_slice_in_dim(
        qkv_sums.reshape(-1), linear * qkv_bias.shape[1], qkv_bias.shape[1]
    )
    owner_up_bias = lax.dynamic_slice_in_dim(
        up_sums.reshape(-1), linear * up_bias.shape[1], up_bias.shape[1]
    )
    bias_sums = add_small(jnp.sum(grad_all.astype(F32), axis=0), ("bi",))
    owner_out_bias = lax.dynamic_slice_in_dim(
        bias_sums, linear * proj_bias.shape[1], proj_bias.shape[1]
    )
    norm_sums = add_small(jnp.stack([grad_gain, grad_shift]), every)
    owner_norm = lax.dynamic_slice_in_dim(
        norm_sums, linear * norm_gain.shape[1], norm_gain.shape[1], axis=1
    )
    return (
        updated.astype(BF16).reshape(tokens.shape),
        grad_tokens.reshape(tokens.shape),
        owner_norm[:1],
        owner_norm[1:],
        owner_qkv[None],
        owner_qkv_bias[None],
        owner_proj[None],
        owner_out_bias[None],
        owner_up[None],
        owner_up_bias[None],
        owner_down[None],
        owner_out_bias[None],
    )


def solution(mesh):
    n_batch, n_ctx = mesh.shape["batch"], mesh.shape["ctx"]
    n_bo = max(1, min(n_batch, D // LANES // n_ctx))
    n_cc = 2 if n_ctx % 2 == 0 else 1
    shape = (n_bo, n_batch // n_bo, n_ctx // n_cc, n_cc)
    inner = Mesh(mesh.devices.reshape(shape), ("bo", "bi", "cy", "cc"))
    batch, ctx = ("bo", "bi"), ("cy", "cc")
    both = batch + ctx
    rows = P(batch, ctx, None)
    vector = P(None, both)
    tall = P(None, both, None)
    wide = P(None, ctx, batch)
    return jax.shard_map(
        body,
        mesh=inner,
        in_specs=(
            rows,
            P(batch, ctx),
            P(batch, ctx),
            vector,
            vector,
            tall,
            vector,
            wide,
            vector,
            tall,
            vector,
            wide,
            vector,
            rows,
        ),
        out_specs=(
            rows,
            rows,
            vector,
            vector,
            tall,
            vector,
            wide,
            vector,
            tall,
            vector,
            wide,
            vector,
        ),
        check_vma=False,
    )
```
